32 devices in a mesh: row: 8 (over z, x), col: 4 (over y, core).
Axes of the slice: x: 2, y: 2, z: 4, core: 2. Of those that a mesh axis runs over, the one named last changes fastest.
Arguments:
- query_tiles: bfloat16 [512, 512, 512], P('row', 'col'), may hold values from -12 to 12
- key_tiles: bfloat16 [512, 512, 512], P('row', 'col'), may hold values from -12 to 12
- value_tiles: bfloat16 [512, 512, 512], P('row', 'col'), may hold values from -6 to 6
- out_grad: bfloat16 [512, 512, 512], P('row', 'col'), may hold values from -6 to 6
Outputs:
- attended: bfloat16 [512, 512, 512], P('row', 'col')
- query_grad: bfloat16 [512, 512, 512], P('row', 'col')
- key_grad: bfloat16 [512, 512, 512], P('row', 'col')
- value_grad: bfloat16 [512, 512, 512], P('row', 'col')
The draws below stay inside these ranges and needn't reach their ends.
All inputs are finite; a program needn't handle non-finite values.
Results may differ from the reference program's by a relative error of at most 0.015.
Values may be sent and summed in bfloat16 or wider, within the bound.
No kernel may reach another device: no remote copies, remote signals or barrier semaphores. Data moves between devices by JAX's collectives and lax.ppermute only.
A program may use at most 448 MiB of HBM per device.

```python
from functools import partial
import jax
import jax.numpy as jnp
from jax import lax

G = 512
H = 4
E = 128


def base_field(key):
    return jnp.clip(jax.random.normal(key, (G, G, H * E), jnp.float32), -6.0, 6.0)


def draw_query_tiles(key, part):
    values_field = base_field(jax.random.fold_in(key, 1))
    return values_field.astype(jnp.bfloat16)


def draw_key_tiles(key, part):
    values_field = base_field(jax.random.fold_in(key, 2))
    return values_field.astype(jnp.bfloat16)


def block_levels(rng, dims, pieces, smallest, high):
    factor_of = 1.0
    for dim, shards_of in pieces:
        draws = jax.random.uniform(jax.random.fold_in(jax.random.fold_in(rng, 6), dim), (shards_of,), jnp.float32, smallest / len(pieces), high / len(pieces))
        factor_of = factor_of * jnp.repeat(jnp.exp(draws), dims[dim] // shards_of).reshape((-1,) + (1,) * (len(dims) - 1 - dim))
    return factor_of


def noise(rng, shape, spread, most, split=(), kind=jnp.bfloat16):
    values = spread * jax.random.normal(rng, shape, jnp.float32)
    if split:
        values = values * block_levels(rng, shape, split, -0.22, 0.18)
    return jnp.clip(values, -most, most).astype(kind)


def setup_inputs(seed: int = 0) -> dict:
    streams_of = jax.random.split(jax.random.key(seed), 5)
    query_tiles = draw_query_tiles(jax.random.fold_in(streams_of[4], 71), 0)
    key_tiles = draw_key_tiles(jax.random.fold_in(streams_of[4], 71), 0)
    value_tiles = noise(streams_of[2], (G, G, H * E), 1.0, 6.0, ((0, 8), (1, 4)))
    out_grad = noise(streams_of[3], (G, G, H * E), 1.0, 6.0, ((0, 8), (1, 4)))
    return dict(query_tiles=query_tiles, key_tiles=key_tiles, value_tiles=value_tiles, out_grad=out_grad)


NEG_FILL = -1.0e30


def round_half(values_in):
    return lax.optimization_barrier(values_in.astype(jnp.bfloat16)).astype(jnp.float32)


def causal_mask(length, strict):
    query_pos = lax.broadcasted_iota(jnp.int32, (length, length), 0)
    key_pos = lax.broadcasted_iota(jnp.int32, (length, length), 1)
    if strict:
        return key_pos < query_pos
    return key_pos <= query_pos


def split_heads(array_in):
    return array_in.astype(jnp.float32).reshape(array_in.shape[0], G, H, E)


def part_forward(query_rows, key_rows, value_rows, strict):
    batch_count = query_rows.shape[0]
    query_heads = split_heads(query_rows)
    key_heads = split_heads(key_rows)
    value_heads = split_heads(value_rows)
    scores = jnp.einsum("bqhe,bkhe->bhqk", query_heads, key_heads) * (E ** -0.5)
    causal = causal_mask(G, strict)
    top_score = jnp.max(jnp.where(causal, scores, NEG_FILL), axis=-1)
    weights = jnp.where(causal, jnp.exp(scores - top_score[..., None]), 0.0)
    weight_sum = jnp.maximum(jnp.sum(weights, axis=-1), 1.0)
    numerator = jnp.einsum("bhqk,bkhe->bqhe", round_half(weights), value_heads)
    partial_out = numerator / jnp.transpose(weight_sum, (0, 2, 1))[..., None]
    log_total = jnp.transpose(top_score + jnp.log(weight_sum), (0, 2, 1))
    return partial_out.reshape(batch_count, G, H * E).astype(jnp.bfloat16), log_total


def part_backward(query_rows, key_rows, value_rows, grad_rows, log_total, grad_dot, strict):
    batch_count = query_rows.shape[0]
    query_heads = split_heads(query_rows)
    key_heads = split_heads(key_rows)
    value_heads = split_heads(value_rows)
    grad_heads = split_heads(grad_rows)
    scale_factor = E ** -0.5
    scores = jnp.einsum("bqhe,bkhe->bhqk", query_heads, key_heads) * scale_factor
    causal = causal_mask(G, strict)
    total_back = jnp.transpose(log_total, (0, 2, 1))
    weights = jnp.where(causal, jnp.exp(scores - total_back[..., None]), 0.0)
    weight_grad = jnp.einsum("bqhe,bkhe->bhqk", grad_heads, value_heads)
    score_grad = weights * (weight_grad - jnp.transpose(grad_dot, (0, 2, 1))[..., None])
    weights_half = round_half(weights)
    score_half = round_half(score_grad)
    value_grad = jnp.einsum("bhqk,bqhe->bkhe", weights_half, grad_heads)
    query_grad = jnp.einsum("bhqk,bkhe->bqhe", score_half, key_heads) * scale_factor
    key_grad = jnp.einsum("bhqk,bqhe->bkhe", score_half, query_heads) * scale_factor
    return (query_grad.reshape(batch_count, G, H * E).astype(jnp.bfloat16),
            key_grad.reshape(batch_count, G, H * E).astype(jnp.bfloat16),
            value_grad.reshape(batch_count, G, H * E).astype(jnp.bfloat16))


def blockwise(function, arrays):
    shaped = tuple(array_in.reshape((G // 16, 16) + array_in.shape[1:]) for array_in in arrays)
    outcome = lax.map(lambda grouped_in: function(*grouped_in), shaped)
    return tuple(result.reshape((G,) + result.shape[2:]) for result in outcome)


def reference(query_tiles, key_tiles, value_tiles, out_grad):
    out_row, total_row = blockwise(partial(part_forward, strict=False), (query_tiles, key_tiles, value_tiles))
    swapped = tuple(jnp.swapaxes(array_in, 0, 1) for array_in in (query_tiles, key_tiles, value_tiles, out_grad))
    out_col, total_col = blockwise(partial(part_forward, strict=True), swapped[:3])
    total_col_t = jnp.swapaxes(total_col, 0, 1)
    top_total = jnp.maximum(total_row, total_col_t)
    log_total = top_total + jnp.log(jnp.exp(total_row - top_total) + jnp.exp(total_col_t - top_total))
    share_row = jnp.exp(total_row - log_total)
    share_col = jnp.exp(total_col_t - log_total)
    part_row = out_row.astype(jnp.float32).reshape(G, G, H, E)
    part_col = jnp.swapaxes(out_col, 0, 1).astype(jnp.float32).reshape(G, G, H, E)
    weighted_row = round_half(share_row[..., None] * part_row)
    weighted_col = round_half(share_col[..., None] * part_col)
    attended = (weighted_row + weighted_col).reshape(G, G, H * E).astype(jnp.bfloat16)
    merged = share_row[..., None] * part_row + share_col[..., None] * part_col
    grad_dot = jnp.sum(out_grad.astype(jnp.float32).reshape(G, G, H, E) * merged, axis=-1)
    grads_row = blockwise(partial(part_backward, strict=False),
                          (query_tiles, key_tiles, value_tiles, out_grad, log_total, grad_dot))
    grads_col = blockwise(partial(part_backward, strict=True),
                          swapped + (jnp.swapaxes(log_total, 0, 1), jnp.swapaxes(grad_dot, 0, 1)))
    summed = tuple((grads_row[member].astype(jnp.float32)
                    + jnp.swapaxes(grads_col[member], 0, 1).astype(jnp.float32)).astype(jnp.bfloat16)
                   for member in range(3))
    return attended, summed[0], summed[1], summed[2]
```

```python
import jax
import jax.numpy as jnp
from jax import lax
from jax.experimental import pallas as pl
from jax.experimental.pallas import tpu as pltpu
from jax.sharding import PartitionSpec as P

H = 4
GROUPS = 4
NEG = -1e30
FLOOR = -1e29
LOG2E = 1.4426950408889634
BF = jnp.bfloat16
F32 = jnp.float32


def nt(a, b):
    return lax.dot_general(a, b, (((1,), (1,)), ((), ())), preferred_element_type=F32)


def nn(a, b):
    return lax.dot_general(a, b, (((1,), (0,)), ((), ())), preferred_element_type=F32)


def tn(a, b):
    return lax.dot_general(a, b, (((0,), (0,)), ((), ())), preferred_element_type=F32)


def cat(parts, axis):
    return parts[0] if len(parts) == 1 else jnp.concatenate(parts, axis=axis)


class Plan:
    def __init__(self, row_count, col_count, tile_shape):
        self.R, self.C = row_count, col_count
        self.I = row_count // GROUPS
        self.nr, self.nc, width = tile_shape
        self.E = width // H
        self.W = self.nc // self.I
        self.W2 = self.W // 2
        self.B = self.nr * self.I
        self.G = self.nc * col_count
        self.nrr = self.nr // col_count
        self.CB = min(8, self.W2)
        assert self.I * GROUPS == row_count
        for n in (self.R, self.C, self.nr, self.nc):
            assert n & (n - 1) == 0
        e = self.E
        self.scale = e ** -0.5
        self.scale2 = self.scale * LOG2E


def pack_columns(pn, sp, arrays, h):
    nr, W2, CB, E, I = pn.nr, pn.W2, pn.CB, pn.E, pn.I
    keys = [(s, half) for s in range(I) for half in range(2)]

    def spec(s, half):
        def index(j, sp):
            i, low = sp[1], sp[0] >= GROUPS // 2
            off = jnp.where(low, 1 - half, half)
            return (0, ((i ^ s) * 2 + off) * (W2 // CB) + j, h)

        return pl.BlockSpec((nr, CB, E), index)

    def body(sp, *refs):
        ins, outs = refs[: 4 * len(keys)], refs[4 * len(keys) :]

        def run(mover, stayer):
            for n, (s, half) in enumerate(keys):
                for kind in range(2):
                    outs[3 * s + half][kind] = jnp.swapaxes(ins[4 * n + mover[kind]][...], 0, 1)
                    outs[3 * s + 2][half, kind] = jnp.swapaxes(
                        ins[4 * n + stayer[kind]][...], 0, 1
                    )

        @pl.when(sp[0] < GROUPS // 2)
        def _():
            run((1, 2), (0, 3))

        @pl.when(sp[0] >= GROUPS // 2)
        def _():
            run((0, 3), (1, 2))

    mover_spec = pl.BlockSpec((2, CB, nr, E), lambda j, sp: (0, j, 0, 0))
    stay_spec = pl.BlockSpec((2, 2, CB, nr, E), lambda j, sp: (0, 0, j, 0, 0))
    mover = jax.ShapeDtypeStruct((2, W2, nr, E), BF)
    stay = jax.ShapeDtypeStruct((2, 2, W2, nr, E), BF)
    outs = pl.pallas_call(
        body,
        name="pack_columns",
        grid_spec=pltpu.PrefetchScalarGridSpec(
            num_scalar_prefetch=1,
            grid=(W2 // CB,),
            in_specs=[spec(s, half) for s, half in keys for _ in range(4)],
            out_specs=[mover_spec, mover_spec, stay_spec] * I,
        ),
        out_shape=[mover, mover, stay] * I,
    )(sp, *[a for _ in keys for a in arrays])
    return [outs[3 * s] for s in range(I)], [outs[3 * s + 1] for s in range(I)], [
        outs[3 * s + 2] for s in range(I)
    ]


def pack_rows(pn, sp, arrays, h):
    nrr, nc, E, C = pn.nrr, pn.nc, pn.E, pn.C
    rb = min(4, nrr)

    def spec(s):
        return pl.BlockSpec(
            (rb, nc, E), lambda j, sp: ((sp[2] ^ s) * (nrr // rb) + j, 0, h)
        )

    def body(sp, *refs):
        for s in range(C):
            for a in range(4):
                refs[4 * C + s][a] = refs[4 * s + a][...]

    return pl.pallas_call(
        body,
        name="pack_rows",
        grid_spec=pltpu.PrefetchScalarGridSpec(
            num_scalar_prefetch=1,
            grid=(nrr // rb,),
            in_specs=[spec(s) for s in range(C) for _ in range(4)],
            out_specs=[pl.BlockSpec((4, rb, nc, E), lambda j, sp: (0, j, 0, 0))] * C,
        ),
        out_shape=[jax.ShapeDtypeStruct((4, nrr, nc, E), BF)] * C,
    )(sp, *[a for _ in range(C) for a in arrays])


def unpack(pn, sp, h, movers_send, movers_keep, stayers, row_pieces, tiles):
    nr, nc, nrr, W2, CB, E, I, C = pn.nr, pn.nc, pn.nrr, pn.W2, pn.CB, pn.E, pn.I, pn.C
    keys = [(s, half) for s in range(I) for half in range(2)]
    steps = W2 // CB

    def column(g, j, sp):
        s, half = g // 2, g % 2
        off = jnp.where(sp[0] >= GROUPS // 2, 1 - half, half)
        return ((sp[1] ^ s) * 2 + off) * steps + j

    def mover_index(n):
        return lambda g, j, sp: (0, jnp.where(g == n, j, jnp.where(g < n, 0, steps - 1)), 0, 0)

    def stay_index(s):
        def index(g, j, sp):
            inside = g // 2 == s
            before = g // 2 < s
            return (
                jnp.where(inside, g % 2, jnp.where(before, 0, 1)),
                0,
                jnp.where(inside, j, jnp.where(before, 0, steps - 1)),
                0,
                0,
            )

        return index

    in_specs = (
        [pl.BlockSpec((2, CB, nr, E), mover_index(n)) for n in range(len(keys))]
        + [pl.BlockSpec((1, 2, CB, nr, E), stay_index(s)) for s in range(I)]
        + [
            pl.BlockSpec((4, nrr, CB, E), lambda g, j, sp: (0, 0, column(g, j, sp), 0))
            for _ in range(C)
        ]
    )
    operands = (
        [x for s in range(I) for x in (movers_send[s], movers_keep[s])]
        + list(stayers)
        + list(row_pieces)
    )
    aliases = {}
    if tiles is not None:
        for k in range(4):
            aliases[1 + len(operands) + k] = k
        in_specs = in_specs + [pl.BlockSpec(memory_space=pl.ANY)] * 4
        operands = operands + list(tiles)
    n_keys = len(keys)

    def body(sp, *refs):
        outs = refs[len(in_specs) : len(in_specs) + 4]
        row_acc = refs[len(in_specs) + 4]
        rows = refs[n_keys + I : n_keys + I + C]
        for s in range(C):
            base = (sp[2] ^ s) * nrr
            for k in range(4):
                row_acc[k, pl.ds(base, nrr)] = rows[s][k].astype(F32)
        g = pl.program_id(0)
        for n, (s, half) in enumerate(keys):

            def run(mover, stayer, n=n, s=s):
                for kind in range(2):
                    for ref, out in (
                        (refs[n].at[kind], mover[kind]),
                        (refs[n_keys + s].at[0, kind], stayer[kind]),
                    ):
                        turned = jnp.swapaxes(ref[...], 0, 1).astype(F32)
                        outs[out][...] = (row_acc[out] + turned).astype(BF)

            @pl.when((g == n) & (sp[0] < GROUPS // 2))
            def _():
                run((2, 3), (1, 0))

            @pl.when((g == n) & (sp[0] >= GROUPS // 2))
            def _():
                run((1, 0), (2, 3))

    out_spec = pl.BlockSpec((nr, CB, E), lambda g, j, sp: (0, column(g, j, sp), h))
    return pl.pallas_call(
        body,
        name="unpack",
        grid_spec=pltpu.PrefetchScalarGridSpec(
            num_scalar_prefetch=1,
            grid=(len(keys), steps),
            in_specs=in_specs,
            out_specs=[out_spec] * 4,
            scratch_shapes=[pltpu.VMEM((4, nr, CB, E), F32)],
        ),
        out_shape=[jax.ShapeDtypeStruct((nr, nc, E * H), BF)] * 4,
        input_output_aliases=aliases,
    )(sp, *operands)


def column_roles(keep):
    if keep:
        return [
            (("S",), ("M",)),
            (("S", "P", "PR"), ("O", "M")),
            (("M", "O"), ("PR", "P", "S")),
            (("M",), ("S",)),
        ]
    return [
        (("S",), ("M",)),
        (("S",), ("O", "M")),
        (("M", "O"), ("S",)),
        (("M",), ("S",)),
    ]


def diag_mask(pn, i):
    shape = (pn.B, pn.B)
    flip = i * pn.nr
    key = lax.broadcasted_iota(jnp.int32, shape, 0) ^ flip
    query = lax.broadcasted_iota(jnp.int32, shape, 1) ^ flip
    return key < query


def masked_scores(pn, keys, queries, mask):
    B = pn.B
    full = nt(keys, queries) * pn.scale2
    last = keys.shape[0] - B
    corner = jnp.where(mask, full[last:, :B], NEG)
    bottom = cat([corner, full[last:, B:]], 1) if queries.shape[0] > B else corner
    return cat([full[:last], bottom], 0) if last else bottom


def column_inputs(pn, keep, M, S, O, P_=None, PR=None):
    nr, E, CB, I = pn.nr, pn.E, pn.CB, pn.I
    mover = pl.BlockSpec((2, CB, nr, E), lambda j, sp: (0, j, 0, 0))
    half = 1 if keep else 0
    stay = pl.BlockSpec((None, 2, CB, nr, E), lambda j, sp: (half, 0, j, 0, 0))
    names, operands, specs = [], [], []
    for name, group, spec in (
        ("M", M, mover),
        ("S", S, stay),
        ("O", O, mover),
        ("P", P_, mover),
        ("PR", PR, mover),
    ):
        if group is not None:
            names.append(name)
            operands += list(group)
            specs += [spec] * I
    return names, operands, specs


def stat_fill(ref, slot, w, pn):
    ref[slot, 0, pl.ds(w, 1), :] = jnp.full((1, pn.B), FLOOR, F32)
    ref[slot, 1, pl.ds(w, 1), :] = jnp.zeros((1, pn.B), F32)


def column_forward(pn, sp, keep, M, S, O, P_=None, PR=None):
    B, CB, W2, I = pn.B, pn.CB, pn.W2, pn.I
    names, operands, specs = column_inputs(pn, keep, M, S, O, P_, PR)
    roles = column_roles(keep)

    def body(sp, *refs):
        groups = {name: refs[n * I : (n + 1) * I] for n, name in enumerate(names)}
        out = refs[len(names) * I]
        mask = diag_mask(pn, sp[1])

        def block(name, kind, w):
            return [r[kind, w] for r in groups[name]]

        def gather(sources, kind, w):
            return cat([p for name in sources for p in block(name, kind, w)], 0)

        def one(w, queries, keys):
            q, g = gather(queries, 0, w), gather(queries, 1, w)
            k, v = gather(keys, 0, w), gather(keys, 1, w)
            scores = masked_scores(pn, k, q, mask)
            top = jnp.maximum(jnp.max(scores, axis=0, keepdims=True), FLOOR)
            weights = jnp.exp2(scores - top)
            total = jnp.maximum(jnp.sum(weights, axis=0, keepdims=True), 1.0)
            dot = jnp.sum(weights * nt(v, g), axis=0, keepdims=True) / total
            lse = top + jnp.log2(total)
            for slot in range(3):
                if slot < len(queries):
                    out[slot, 0, pl.ds(w, 1), :] = lse[:, slot * B : (slot + 1) * B]
                    out[slot, 1, pl.ds(w, 1), :] = dot[:, slot * B : (slot + 1) * B]
                else:
                    stat_fill(out, slot, w, pn)

        for z, (queries, keys) in enumerate(roles):

            @pl.when(sp[0] == z)
            def _(queries=queries, keys=keys):
                def step(w, carry):
                    one(w, queries, keys)
                    return carry

                lax.fori_loop(0, CB, step, 0, unroll=2)

    return pl.pallas_call(
        body,
        name="column_forward",
        grid_spec=pltpu.PrefetchScalarGridSpec(
            num_scalar_prefetch=1,
            grid=(W2 // CB,),
            in_specs=specs,
            out_specs=pl.BlockSpec((3, 2, CB, B), lambda j, sp: (0, 0, j, 0)),
        ),
        out_shape=jax.ShapeDtypeStruct((3, 2, W2, B), F32),
    )(sp, *operands)


def column_backward(pn, sp, keep, totals, M, S, O, P_=None, PR=None):
    B, CB, W2, I, nr, E = pn.B, pn.CB, pn.W2, pn.I, pn.nr, pn.E
    names, operands, specs = column_inputs(pn, keep, M, S, O, P_, PR)
    roles = column_roles(keep)
    n_tot = len(totals)
    tot_spec = pl.BlockSpec((2, CB, B), lambda j, sp: (0, j, 0))
    grad = pl.BlockSpec((2, CB, nr, E), lambda j, sp: (0, j, 0, 0))

    def body(sp, *refs):
        n_in = len(names) * I
        groups = {name: refs[n * I : (n + 1) * I] for n, name in enumerate(names)}
        tots = refs[n_in : n_in + n_tot]
        first = n_in + n_tot
        outs = {
            name: refs[first + n * I : first + (n + 1) * I] for n, name in enumerate(names)
        }
        mask = diag_mask(pn, sp[1])

        def gather(sources, kind, w):
            return cat([r[kind, w] for name in sources for r in groups[name]], 0)

        def scatter(sources, kind, w, value):
            for n, name in enumerate(sources):
                for s in range(I):
                    base = n * B + s * nr
                    outs[name][s][kind, w] = value[base : base + nr].astype(BF)

        def one(w, queries, keys):
            q, g = gather(queries, 0, w), gather(queries, 1, w)
            k, v = gather(keys, 0, w), gather(keys, 1, w)
            logs = cat([tots[n][0, pl.ds(w, 1), :] for n in range(len(queries))], 1)
            dots = cat([tots[n][1, pl.ds(w, 1), :] for n in range(len(queries))], 1)
            probs = jnp.exp2(masked_scores(pn, k, q, mask) - logs)
            ds = (probs * (nt(v, g) - dots)).astype(BF)
            probs = probs.astype(BF)
            scatter(keys, 1, w, nn(probs, g))
            scatter(keys, 0, w, nn(ds, q) * pn.scale)
            scatter(queries, 0, w, tn(ds, k) * pn.scale)
            scatter(queries, 1, w, tn(probs, v))

        for z, (queries, keys) in enumerate(roles):

            @pl.when(sp[0] == z)
            def _(queries=queries, keys=keys):
                def step(w, carry):
                    one(w, queries, keys)
                    return carry

                lax.fori_loop(0, CB, step, 0, unroll=2)

    shape = jax.ShapeDtypeStruct((2, W2, nr, E), BF)
    outs = pl.pallas_call(
        body,
        name="column_backward",
        grid_spec=pltpu.PrefetchScalarGridSpec(
            num_scalar_prefetch=1,
            grid=(W2 // CB,),
            in_specs=specs + [tot_spec] * n_tot,
            out_specs=[grad] * (len(names) * I),
        ),
        out_shape=[shape] * (len(names) * I),
    )(sp, *operands, *totals)
    return {name: list(outs[n * I : (n + 1) * I]) for n, name in enumerate(names)}


def row_block(pn):
    return min(256, pn.G)


def row_scores(pn, k, q, base, size):
    full = nt(k[base : base + size], q[base:]) * pn.scale2
    key = lax.broadcasted_iota(jnp.int32, (size, size), 0)
    query = lax.broadcasted_iota(jnp.int32, (size, size), 1)
    corner = jnp.where(key <= query, full[:, :size], NEG)
    return cat([corner, full[:, size:]], 1) if base + size < pn.G else corner


def assemble(pn, sp, pieces, scratch):
    for s in range(pn.C):
        base = pl.multiple_of((sp[2] ^ s) * pn.nc, pn.nc)
        for kind in range(4):
            scratch[kind, pl.ds(base, pn.nc), :] = pieces[s][kind, 0]


def row_forward(pn, sp, pieces):
    nrr, nc, C, G, E = pn.nrr, pn.nc, pn.C, pn.G, pn.E
    KB = row_block(pn)

    def body(sp, *refs):
        out, scratch = refs[C], refs[C + 1]
        assemble(pn, sp, refs[:C], scratch)
        q, k, v, g = (scratch[n] for n in range(4))
        blocks = [row_scores(pn, k, q, base, KB) for base in range(0, G, KB)]

        def fold(values, join):
            total = values[0]
            for n in range(1, len(values)):
                at = n * KB
                total = cat([total[:, :at], join(total[:, at:], values[n])], 1)
            return total

        top = fold([jnp.max(b, axis=0, keepdims=True) for b in blocks], jnp.maximum)
        weights = [jnp.exp2(b - top[:, n * KB :]) for n, b in enumerate(blocks)]
        total = fold([jnp.sum(w, axis=0, keepdims=True) for w in weights], jnp.add)
        total = jnp.maximum(total, 1.0)
        dots = [
            jnp.sum(w * nt(v[n * KB : (n + 1) * KB], g[n * KB :]), axis=0, keepdims=True)
            for n, w in enumerate(weights)
        ]
        dot = fold(dots, jnp.add) / total
        lse = top + jnp.log2(total)
        r = pl.program_id(0)
        for n in range(C):
            out[n ^ sp[2], 0, pl.ds(r, 1), :] = lse[:, n * nc : (n + 1) * nc]
            out[n ^ sp[2], 1, pl.ds(r, 1), :] = dot[:, n * nc : (n + 1) * nc]

    return pl.pallas_call(
        body,
        name="row_forward",
        grid_spec=pltpu.PrefetchScalarGridSpec(
            num_scalar_prefetch=1,
            grid=(nrr,),
            in_specs=[pl.BlockSpec((4, 1, nc, E), lambda r, sp: (0, r, 0, 0))] * C,
            out_specs=pl.BlockSpec((C, 2, nrr, nc), lambda r, sp: (0, 0, 0, 0)),
            scratch_shapes=[pltpu.VMEM((4, G, E), BF)],
        ),
        out_shape=jax.ShapeDtypeStruct((C, 2, nrr, nc), F32),
    )(sp, *pieces)


def row_backward(pn, sp, pieces, totals):
    nrr, nc, C, G, E = pn.nrr, pn.nc, pn.C, pn.G, pn.E
    KB = row_block(pn)

    def body(sp, *refs):
        tots, outs = refs[C : 2 * C], refs[2 * C : 3 * C]
        scratch, stat, acc = refs[3 * C :]
        r = pl.program_id(0)
        assemble(pn, sp, refs[:C], scratch)
        for s in range(C):
            for kind in range(2):
                stat[kind, pl.ds(sp[2] ^ s, 1), :] = tots[s][kind, pl.ds(r, 1), :]
        q, k, v, g = (scratch[n] for n in range(4))
        logs = cat([stat[0, n : n + 1, :] for n in range(C)], 1)
        dots = cat([stat[1, n : n + 1, :] for n in range(C)], 1)
        for base in range(0, G, KB):
            kb, vb = k[base : base + KB], v[base : base + KB]
            qb, gb = q[base:], g[base:]
            probs = jnp.exp2(row_scores(pn, k, q, base, KB) - logs[:, base:])
            ds = (probs * (nt(vb, gb) - dots[:, base:])).astype(BF)
            probs = probs.astype(BF)
            acc[2, base : base + KB, :] = nn(ds, qb) * pn.scale
            acc[3, base : base + KB, :] = nn(probs, gb)
            if base == 0:
                acc[1] = tn(ds, kb)
                acc[0] = tn(probs, vb)
            else:
                acc[1, base:, :] += tn(ds, kb)
                acc[0, base:, :] += tn(probs, vb)
        for s in range(C):
            at = pl.ds(pl.multiple_of((sp[2] ^ s) * nc, nc), nc)
            outs[s][0, 0] = acc[0, at, :].astype(BF)
            outs[s][1, 0] = (acc[1, at, :] * pn.scale).astype(BF)
            outs[s][2, 0] = acc[2, at, :].astype(BF)
            outs[s][3, 0] = acc[3, at, :].astype(BF)

    piece = pl.BlockSpec((4, 1, nc, E), lambda r, sp: (0, r, 0, 0))
    return pl.pallas_call(
        body,
        name="row_backward",
        grid_spec=pltpu.PrefetchScalarGridSpec(
            num_scalar_prefetch=1,
            grid=(nrr,),
            in_specs=[piece] * C + [pl.BlockSpec((2, nrr, nc), lambda r, sp: (0, 0, 0))] * C,
            out_specs=[piece] * C,
            scratch_shapes=[
                pltpu.VMEM((4, G, E), BF),
                pltpu.VMEM((2, max(8, C), nc), F32),
                pltpu.VMEM((4, G, E), F32),
            ],
        ),
        out_shape=[jax.ShapeDtypeStruct((4, nrr, nc, E), BF)] * C,
    )(sp, *pieces, *totals)


class Moves:
    def __init__(self, pn):
        I, C, Z = pn.I, pn.C, GROUPS
        self.at = lambda z, i: z * I + i
        inner = range(I)
        self.out_to_in = self.pairs(((0, 1), (3, 2)), inner)
        self.in_to_out = self.pairs(((1, 0), (2, 3)), inner)
        self.swap_in = self.pairs(((1, 2), (2, 1)), inner)
        self.up1 = self.pairs(((1, 2), (2, 3)), inner)
        self.up2 = self.pairs(((1, 3),), inner)
        self.down1 = self.pairs(((3, 2), (2, 1)), inner)
        self.down2 = self.pairs(((3, 1),), inner)
        self.inner = [
            [(self.at(z, i), self.at(z, i ^ s)) for z in range(Z) for i in inner]
            for s in range(I)
        ]
        self.cols = [[(c, c ^ s) for c in range(C)] for s in range(C)]

    def pairs(self, zs, inner):
        return [(self.at(a, i), self.at(b, i)) for a, b in zs for i in inner]

    def z(self, values, pairs):
        if isinstance(values, (list, tuple)):
            return [lax.ppermute(v, "row", pairs) for v in values]
        return lax.ppermute(values, "row", pairs)

    def over_inner(self, pieces):
        return [
            p if s == 0 else lax.ppermute(p, "row", self.inner[s]) for s, p in enumerate(pieces)
        ]

    def over_cols(self, pieces):
        return [
            p if s == 0 else lax.ppermute(p, "col", self.cols[s]) for s, p in enumerate(pieces)
        ]


def add_half(a, b):
    return (a.astype(F32) + b.astype(F32)).astype(BF)


def merge(parts):
    top = parts[0][0]
    for p in parts[1:]:
        top = jnp.maximum(top, p[0])
    shares = [jnp.exp2(p[0] - top) for p in parts]
    total = sum(shares)
    dot = sum(w * p[1] for w, p in zip(shares, parts)) / total
    return jnp.stack([top + jnp.log2(total), dot])


def shards(query_tiles, key_tiles, value_tiles, out_grad):
    row_count, col_count = lax.axis_size("row"), lax.axis_size("col")
    pn = Plan(row_count, col_count, query_tiles.shape)
    mv = Moves(pn)
    I, C, W, W2, B, nr, nc, nrr = pn.I, pn.C, pn.W, pn.W2, pn.B, pn.nr, pn.nc, pn.nrr
    row_at = lax.axis_index("row")
    z, i, c = row_at // I, row_at % I, lax.axis_index("col")
    sp = jnp.stack([z, i, c]).astype(jnp.int32)
    arrays = (query_tiles, key_tiles, value_tiles, out_grad)
    low = z >= GROUPS // 2

    def half_start(s, half):
        off = jnp.where(low, 1 - half, half)
        return ((i ^ s) * 2 + off) * W2

    neutral = jnp.stack([jnp.full((W2, B), FLOOR, F32), jnp.zeros((W2, B), F32)])
    inputs, stats = [], []
    for h in range(H):
        Ms, Mk, S = pack_columns(pn, sp, arrays, h)
        rows = pack_rows(pn, sp, arrays, h)
        Ms = mv.over_inner(Ms)
        Os = mv.z(Ms, mv.out_to_in)
        Ps = mv.z(Ms, mv.swap_in)
        PR = mv.z(Os, mv.swap_in)
        Mk = mv.over_inner(Mk)
        Ok = mv.z(Mk, mv.out_to_in)
        S = mv.over_inner(S)
        rows = mv.over_cols(rows)
        inputs.append((Ms, Mk, S, Os, Ok, Ps, PR, rows))

    tiles = None
    for h in range(H):
        Ms, Mk, S, Os, Ok, Ps, PR, rows = inputs[h]
        row_stat = row_forward(pn, sp, rows)
        keep_stat = column_forward(pn, sp, True, Mk, S, Ok, Ps, PR)
        send_stat = column_forward(pn, sp, False, Ms, S, Os)

        back = mv.over_cols([row_stat[s] for s in range(C)])
        home = jnp.zeros((2, nr, nc), F32)
        for s in range(C):
            home = lax.dynamic_update_slice(home, back[s], (0, (c ^ s) * nrr, 0))
        home = jnp.transpose(home, (0, 2, 1))
        pieces = [
            jnp.stack(
                [lax.dynamic_slice_in_dim(home, half_start(s, half), W2, 1) for half in range(2)]
            )
            for s in range(I)
        ]
        row_col = jnp.concatenate(mv.over_inner(pieces), axis=-1)

        up = mv.z(jnp.stack([send_stat[1], keep_stat[1]]), mv.up1)
        far = mv.z(keep_stat[2], mv.up2)
        up_send = jnp.where(low, jnp.where(z == 2, up[1], up[0]), neutral)
        up_keep = jnp.where(low, jnp.where(z == 2, up[0], up[1]), neutral)
        far = jnp.where(z == 3, far, neutral)
        tot_send = merge([send_stat[0], up_send, far, row_col[0]])
        tot_keep = merge([keep_stat[0], up_keep, row_col[1]])

        both = jnp.stack([tot_send, tot_keep])
        down = mv.z(both, mv.down1)
        down_far = mv.z(tot_send, mv.down2)
        next_send = down[0]
        next_keep = jnp.where(z == 1, down[0], down[1])
        pieces = mv.over_inner([both[..., s * nr : (s + 1) * nr] for s in range(I)])
        home = jnp.zeros((2, nc, nr), F32)
        for s in range(I):
            for half in range(2):
                home = lax.dynamic_update_slice(home, pieces[s][half], (0, half_start(s, half), 0))
        home = jnp.transpose(home, (0, 2, 1))
        row_tot = mv.over_cols(
            [lax.dynamic_slice_in_dim(home, (c ^ s) * nrr, nrr, 1) for s in range(C)]
        )

        keep_grad = column_backward(
            pn, sp, True, [tot_keep, next_keep, down_far], Mk, S, Ok, Ps, PR
        )
        from_P = mv.z(keep_grad["P"], mv.swap_in)
        from_PR = mv.z(keep_grad["PR"], mv.swap_in)
        send_grad = column_backward(pn, sp, False, [tot_send, next_send], Ms, S, Os)
        row_grad = row_backward(pn, sp, rows, row_tot)
        row_grad = mv.over_cols(row_grad)

        grad_O = [add_half(a, b) for a, b in zip(send_grad["O"], from_PR)]
        home_s = mv.z(grad_O, mv.in_to_out)
        home_k = mv.z(keep_grad["O"], mv.in_to_out)
        own = (z == 1) | (z == 2)
        grad_s = [
            add_half(a, jnp.where(own, b, d))
            for a, b, d in zip(send_grad["M"], from_P, home_s)
        ]
        grad_k = [add_half(a, b) for a, b in zip(keep_grad["M"], home_k)]
        grad_S = [jnp.stack([a, b]) for a, b in zip(send_grad["S"], keep_grad["S"])]
        grad_s = mv.over_inner(grad_s)
        grad_k = mv.over_inner(grad_k)
        grad_S = mv.over_inner(grad_S)
        tiles = unpack(pn, sp, h, grad_s, grad_k, grad_S, row_grad, tiles)
    return tuple(tiles)


def solution(mesh):
    spec = P("row", "col", None)
    return jax.shard_map(
        shards, mesh=mesh, in_specs=(spec,) * 4, out_specs=(spec,) * 4, check_vma=False
    )
```
